256 devices in a mesh: row: 8 (over z), col: 32 (over y, x, core).
Axes of the slice: x: 4, y: 4, z: 8, core: 2. Of those that a mesh axis runs over, the one named last changes fastest.
Arguments:
- src_pos: float32 [3, 131072], P(None, 'row'), may hold values from 0 to 10
- tgt_pos: float32 [3, 8192], P(None, 'col'), may hold values from 0 to 20
- src_weight: float32 [131072], P('row'), may hold values from 0.1 to 3
- tgt_weight: float32 [8192], P('col'), may hold values from 0.1 to 3
- src_order: int32 [131072], P('row'), may hold values from 0 to 131071, as said below
- tgt_order: int32 [8192], P('col'), may hold values from 0 to 8191, as said below
- tile_mask: int32 [512, 32], P('row', 'col'), may hold values from 0 to 1, as said below
Outputs:
- src_potential: float32 [131072], P('row')
- tgt_potential: float32 [8192], P('col')
- displacement: float32 [3, 131072], P(None, 'row')
The draws below stay inside these ranges and needn't reach their ends.
Inputs may be any that keep to these rules, and one draw needn't show every extreme that they name: `src_order`: each aligned block of 16384 entries is a permutation of that block's own indices. `tgt_order`: each aligned block of 256 entries is a permutation of that block's own indices. `tile_mask`: every row and every column of the mask holds at least one kept pair.
All inputs are finite; a program needn't handle non-finite values.
Results may differ from the reference program's by a relative error of at most 0.0003.
Values sent between devices are 32-bit elements; how exact they have to be, the bound alone decides.
No kernel may reach another device: no remote copies, remote signals or barrier semaphores. Data moves between devices by JAX's collectives and lax.ppermute only.
A program may use at most 64 MiB of HBM per device.

```python
import jax
import jax.numpy as jnp
from jax import lax

TILE = 256
SRC_DEV = 16384
TGT_DEV = 256
SWEEPS = 2
NSRC = 131072
NTGT = 8192


def block_shuffle(key, count, block_size):
    blocks = count // block_size
    block_keys = jax.random.split(key, blocks)

    def shuffle_one(block_key):
        return jax.random.permutation(block_key, block_size)
    shuffles = jax.vmap(shuffle_one)(block_keys)
    return (shuffles + (jnp.arange(blocks) * block_size)[:, None]).reshape(-1).astype(jnp.int32)


def tile_cells(key, tiles, per_block, salt, spread_top, narrow_low, narrow_top):
    blocks = tiles // per_block
    spread_cells = jax.random.randint(jax.random.fold_in(key, salt), (2, 3, tiles), 0, spread_top, dtype=jnp.int32)
    narrow_cells = jax.random.randint(jax.random.fold_in(key, salt + 1), (2, 3, tiles), narrow_low, narrow_top, dtype=jnp.int32)
    crowded = jax.random.randint(jax.random.fold_in(key, salt + 2), (blocks,), 0, 2, dtype=jnp.int32)
    crowded = jnp.repeat(crowded, per_block)
    return jnp.where(crowded[None, None, :] == 1, narrow_cells, spread_cells)


def source_cells(key):
    return tile_cells(key, NSRC // TILE, SRC_DEV // TILE, 20, 4, 1, 3)


def target_cells(key):
    tiles = NTGT // TILE
    per_block = TGT_DEV // TILE
    cells = tile_cells(key, tiles, per_block, 30, 5, 1, 4)
    far_block = jax.random.randint(jax.random.fold_in(key, 33), (), 0, NTGT // TGT_DEV, dtype=jnp.int32)
    far_tiles = jnp.arange(tiles, dtype=jnp.int32) // per_block == far_block
    return jnp.where(far_tiles[None, None, :], 7, cells)


def clustered(key, cells, order, salt):
    inverse = jnp.argsort(order, stable=True).astype(jnp.int32)
    count = order.shape[0]
    tile_of = inverse // TILE
    branch = jax.random.randint(jax.random.fold_in(key, salt + 2), (count,), 0, 2, dtype=jnp.int32)
    first = jnp.take(cells[0], tile_of, axis=1)
    second = jnp.take(cells[1], tile_of, axis=1)
    own_cells = jnp.where(branch[None, :] == 0, first, second).astype(jnp.float32)
    centre = 1.25 + 2.5 * own_cells
    jitter = jax.random.uniform(jax.random.fold_in(key, salt), (3, count), jnp.float32, -1.25, 1.25)
    return centre + jitter


def draw_src_order(key, part):
    return block_shuffle(jax.random.fold_in(key, 9), NSRC, SRC_DEV)


def draw_tgt_order(key, part):
    return block_shuffle(jax.random.fold_in(key, 10), NTGT, TGT_DEV)


def draw_src_pos(key, part):
    return clustered(key, source_cells(key), draw_src_order(key, part), 41)


def draw_tgt_pos(key, part):
    return clustered(key, target_cells(key), draw_tgt_order(key, part), 51)


def rising_mass(key, count):
    rising = 1.0 + 2.0 * jnp.arange(count, dtype=jnp.float32) / (count - 1)
    factor = jnp.exp(jax.random.uniform(key, (count,), jnp.float32, jnp.log(0.2), 0.0))
    return factor * rising


def draw_src_weight(key, part):
    return rising_mass(jax.random.fold_in(key, 7), NSRC)


def draw_tgt_weight(key, part):
    return rising_mass(jax.random.fold_in(key, 8), NTGT)


def draw_tile_mask(key, part):
    src_tiles = NSRC // TILE
    tgt_tiles = NTGT // TILE
    src_cells = source_cells(key)
    tgt_cells = target_cells(key)
    differ = jnp.abs(src_cells[:, None, :, :, None] - tgt_cells[None, :, :, None, :])
    apart = jnp.min(jnp.max(differ, axis=2), axis=(0, 1))
    kept_pairs = apart <= 1
    row_partner = jax.random.permutation(jax.random.fold_in(key, 14), src_tiles) % tgt_tiles
    col_partner = jax.random.permutation(jax.random.fold_in(key, 15), tgt_tiles) % src_tiles
    forced = (jnp.arange(tgt_tiles)[None, :] == row_partner[:, None]) | (jnp.arange(src_tiles)[:, None] == col_partner[None, :])
    return (kept_pairs | forced).astype(jnp.int32)


def setup_inputs(seed: int = 0) -> dict:
    key_of = jax.random.split(jax.random.key(seed), 8)
    src_pos = draw_src_pos(jax.random.fold_in(key_of[7], 71), 0)
    tgt_pos = draw_tgt_pos(jax.random.fold_in(key_of[7], 71), 0)
    src_weight = draw_src_weight(jax.random.fold_in(key_of[7], 71), 0)
    tgt_weight = draw_tgt_weight(jax.random.fold_in(key_of[7], 71), 0)
    src_order = draw_src_order(jax.random.fold_in(key_of[7], 71), 0)
    tgt_order = draw_tgt_order(jax.random.fold_in(key_of[7], 71), 0)
    tile_mask = draw_tile_mask(jax.random.fold_in(key_of[7], 71), 0)
    return dict(src_pos=src_pos, tgt_pos=tgt_pos, src_weight=src_weight, tgt_weight=tgt_weight, src_order=src_order, tgt_order=tgt_order, tile_mask=tile_mask)


epsilon = 0.4
lowest = -1e30


def reference(src_pos, tgt_pos, src_weight, tgt_weight, src_order, tgt_order, tile_mask):
    sources = jnp.take(src_pos, src_order, axis=1)
    targets = jnp.take(tgt_pos, tgt_order, axis=1)
    src_mass = jnp.take(src_weight, src_order)
    tgt_mass = jnp.take(tgt_weight, tgt_order)
    log_a = jnp.log(src_mass) - jnp.log(jnp.sum(src_mass))
    log_b = jnp.log(tgt_mass) - jnp.log(jnp.sum(tgt_mass))
    tile_rows = NSRC // TILE
    src_blocks = sources.reshape(3, tile_rows, TILE).transpose(1, 0, 2)
    keep_rows = jnp.repeat(tile_mask, TILE, axis=1) > 0

    def one_pass(src_field, tgt_field, with_shift):
        toward_terms = log_b + tgt_field / epsilon
        back_rows = (log_a + src_field / epsilon).reshape(tile_rows, TILE)

        def visit(carried, slices):
            col_top, col_sum = carried
            src_block, back_row, keep_row = slices
            distance = 0.5 * sum((src_block[coordinate][:, None] - targets[coordinate][None, :]) ** 2 for coordinate in range(3))
            toward = toward_terms[None, :] - distance / epsilon
            backward = back_row[:, None] - distance / epsilon
            alive = keep_row[None, :]
            row_top = jnp.max(jnp.where(alive, toward, lowest), axis=1)
            row_exp = jnp.where(alive, jnp.exp(toward - row_top[:, None]), 0.0)
            row_sum = jnp.sum(row_exp, axis=1)
            if with_shift:
                pulled = jnp.dot(row_exp, targets.T, precision=lax.Precision.HIGHEST).T
            else:
                pulled = jnp.zeros((3, TILE), jnp.float32)
            col_peak = jnp.max(jnp.where(alive, backward, lowest), axis=0)
            renewed = jnp.maximum(col_top, col_peak)
            col_sum = col_sum * jnp.exp(col_top - renewed) + jnp.sum(jnp.where(alive, jnp.exp(backward - renewed[None, :]), 0.0), axis=0)
            return (renewed, col_sum), (row_top, row_sum, pulled)

        starting = (jnp.full((NTGT,), lowest, jnp.float32), jnp.zeros((NTGT,), jnp.float32))
        (col_top, col_sum), (row_top, row_sum, pulled) = lax.scan(visit, starting, (src_blocks, back_rows, keep_rows))
        row_top = row_top.reshape(-1)
        row_sum = row_sum.reshape(-1)
        src_new = -epsilon * (row_top + jnp.log(row_sum))
        tgt_new = -epsilon * (col_top + jnp.log(col_sum))
        shift = sources - pulled.transpose(1, 0, 2).reshape(3, -1) / row_sum[None, :]
        return src_new, tgt_new, shift

    zero_src = jnp.zeros((NSRC,), jnp.float32)
    zero_tgt = jnp.zeros((NTGT,), jnp.float32)
    src_field, tgt_field, unused = one_pass(zero_src, zero_tgt, False)
    for sweep_at in range(SWEEPS):
        src_new, tgt_new, unused = one_pass(src_field, tgt_field, False)
        src_field = 0.5 * (src_field + src_new)
        tgt_field = 0.5 * (tgt_field + tgt_new)
    src_potential, tgt_potential, displacement = one_pass(src_field, tgt_field, True)
    return src_potential, tgt_potential, displacement
```

```python
import jax
import jax.numpy as jnp
from jax import lax
from jax.experimental import pallas as pl
from jax.experimental.pallas import tpu as pltpu
from jax.sharding import Mesh
from jax.sharding import PartitionSpec as P

epsilon = 0.4
LOG2E = 1.4426950408889634
LN2 = 0.6931471805599453
ALPHA = LOG2E / epsilon
HALF = 0.5 * ALPHA
UNIT = epsilon * LN2
CENTRE = 7.5
LOWEST = -(2.0**100)
TILE = 256
LANES = 128

ROW = "row"
SPLIT = ("x",)
MERGE = ("y", "core")
COLS = ("y", "x", "core")

BIAS_S, BIAS_T, MASK0, LOG_S, RAW_S, LOG_T = 3, 4, 5, 9, 10, 13


def f32(shape):
    return jax.ShapeDtypeStruct(shape, jnp.float32)


def call(body, outs, scratch=(), smem=()):
    def run(*args):
        specs = [
            pl.BlockSpec(memory_space=pltpu.SMEM if k in smem else pltpu.VMEM)
            for k in range(len(args))
        ]
        return pl.pallas_call(
            body,
            out_shape=outs,
            in_specs=specs,
            out_specs=jax.tree.map(lambda _: pl.BlockSpec(memory_space=pltpu.VMEM), outs),
            scratch_shapes=list(scratch),
            compiler_params=pltpu.CompilerParams(vmem_limit_bytes=48 << 20),
        )(*args)

    return run


def parts(u):
    hi = u.astype(jnp.bfloat16)
    rest = u - hi.astype(jnp.float32)
    mid = rest.astype(jnp.bfloat16)
    low = (rest - mid.astype(jnp.float32)).astype(jnp.bfloat16)
    return hi, mid, low


def right_side(u, out_ref):
    hi, mid, low = parts(u)
    zero = jnp.zeros_like(hi)
    out_ref[...] = jnp.concatenate([hi, mid, hi, mid, low, hi, zero, zero], axis=0)


def left_side(u, out_ref):
    hi, mid, low = (p.astype(jnp.float32) for p in parts(u))
    zero = jnp.zeros_like(hi)
    stacked = jnp.concatenate([hi, hi, mid, mid, hi, low, zero, zero], axis=0)
    for c in range(u.shape[1] // LANES):
        block = stacked[:, c * LANES : (c + 1) * LANES]
        out_ref[c * LANES : (c + 1) * LANES, :] = block.T.astype(jnp.bfloat16)


def with_row(u, at, row):
    rows = lax.broadcasted_iota(jnp.int32, u.shape, 0)
    return jnp.where(rows == at, row, u)


def row_block(left_ref, right, pull_refs=None):
    x = jnp.dot(left_ref[...], right, preferred_element_type=jnp.float32)
    n = x.shape[1]
    x = x.reshape(x.shape[0] // 8, 8, n)
    top = jnp.max(x, axis=0)
    p = jnp.exp2(x - top[None])
    total = jnp.sum(p, axis=0)
    peak = jnp.max(top, axis=0, keepdims=True)
    weight = jnp.exp2(top - peak)
    sums = jnp.sum(total * weight, axis=0, keepdims=True)
    value = peak + jnp.log2(sums)
    if pull_refs is None:
        return value
    means = []
    for d in range(3):
        wide = jnp.concatenate([pull_refs[d]] * (n // LANES), axis=1)
        moved = jnp.sum(p * wide.reshape(-1, 8, n), axis=0)
        means.append(jnp.sum(moved * weight, axis=0, keepdims=True) / sums)
    return value, means


def row_pass(left_ref, right_ref, emit, width=TILE, pull_refs=None):
    blocks = right_ref.shape[1] // width

    def step(b, carry):
        at = pl.multiple_of(b * width, width)
        emit(at, row_block(left_ref, right_ref[:, pl.ds(at, width)], pull_refs))
        return carry

    lax.fori_loop(0, blocks, step, 0)


def col_pass(left_ref, right_ref, top_ref, sum_ref, width=1024):
    m = left_ref.shape[0]
    n = right_ref.shape[1]
    for t in range(m // TILE):
        rows = slice(t * TILE, (t + 1) * TILE)

        def step(b, carry):
            top_old, sum_old = carry
            at = pl.multiple_of(b * width, width)
            x = jnp.dot(
                left_ref[rows, :],
                right_ref[:, pl.ds(at, width)],
                preferred_element_type=jnp.float32,
            )
            cuts = [x[:, k * LANES : (k + 1) * LANES] for k in range(width // LANES)]
            top = top_old
            for cut in cuts:
                top = jnp.maximum(top, cut)
            total = sum_old * jnp.exp2(top_old - top)
            for cut in cuts:
                total = total + jnp.exp2(cut - top)
            return top, total

        start = (
            jnp.full((TILE, LANES), 2.0 * LOWEST, jnp.float32),
            jnp.zeros((TILE, LANES), jnp.float32),
        )
        top, total = lax.fori_loop(0, n // width, step, start)
        top_ref[rows, :] = top
        sum_ref[rows, :] = total
    found = []
    for c in range(m // LANES):
        top = top_ref[c * LANES : (c + 1) * LANES, :].T
        total = sum_ref[c * LANES : (c + 1) * LANES, :].T
        peak = jnp.max(top, axis=0, keepdims=True)
        sums = jnp.sum(total * jnp.exp2(top - peak), axis=0, keepdims=True)
        found.append(peak + jnp.log2(sums))
    return jnp.concatenate(found, axis=1)


def merged(values):
    peak = jnp.max(values, axis=0, keepdims=True)
    return peak + jnp.log2(jnp.sum(jnp.exp2(values - peak), axis=0, keepdims=True))


def lane_gather(table, lanes):
    return jnp.take_along_axis(table, lanes, axis=1, mode="promise_in_bounds")


def pack_targets(pos_ref, weight_ref, order_ref, mask_ref, out_ref):
    order = jnp.bitwise_and(order_ref[...], TILE - 1)
    high = jnp.right_shift(order, 7)
    low = jnp.bitwise_and(order, LANES - 1)
    high8 = jnp.concatenate([high] * 4, axis=0)
    low8 = jnp.concatenate([low] * 4, axis=0)
    found = jnp.zeros((8, LANES), jnp.float32)
    for r in range(2):
        lanes = slice(r * LANES, (r + 1) * LANES)
        lines = [jnp.broadcast_to(pos_ref[d : d + 1, lanes], (2, LANES)) for d in range(3)]
        lines.append(jnp.broadcast_to(weight_ref[r : r + 1, :], (2, LANES)))
        table = jnp.concatenate(lines, axis=0)
        found = jnp.where(high8 == r, lane_gather(table, low8), found)
    tiles = mask_ref.shape[0]
    at = lax.broadcasted_iota(jnp.int32, (tiles, LANES), 0)
    lane = lax.broadcasted_iota(jnp.int32, (tiles, LANES), 1)
    kept = jnp.broadcast_to(mask_ref[...].astype(jnp.float32), (tiles, LANES))
    line = jnp.sum(jnp.where(at == lane, kept, 0.0), axis=0, keepdims=True)
    both = jnp.concatenate([found, jnp.broadcast_to(line, (8, LANES))], axis=0)
    for k in range(out_ref.shape[0]):
        out_ref[k] = both


def first_rows(
    quarter_ref, got_ref, pos_ref, weight_ref, order_ref, src_ref, tgt_ref, out_ref,
    left_ref, right_ref,
):
    quarter = quarter_ref[0]
    n = src_ref.shape[1]
    lines = n // LANES
    groups = lines // 8
    order = order_ref[pl.ds(pl.multiple_of(quarter * lines, 8), lines), :]
    order = jnp.bitwise_and(order, LANES * LANES - 1)
    high = jnp.right_shift(order, 7)
    low = jnp.bitwise_and(order, LANES - 1)
    highs = [high[8 * g : 8 * g + 8] for g in range(groups)]
    lows = [low[8 * g : 8 * g + 8] for g in range(groups)]

    def look(r, found):
        at = pl.multiple_of(r * LANES, LANES)
        tables = [
            jnp.broadcast_to(pos_ref[d : d + 1, pl.ds(at, LANES)], (8, LANES)) for d in range(3)
        ]
        tables.append(jnp.broadcast_to(weight_ref[pl.ds(r, 1), :], (8, LANES)))
        out = []
        for g in range(groups):
            here = highs[g] == r
            for a in range(4):
                old = found[4 * g + a]
                out.append(jnp.where(here, lane_gather(tables[a], lows[g]), old))
        return tuple(out)

    zero = jnp.zeros((8, LANES), jnp.float32)
    found = lax.fori_loop(0, LANES, look, (zero,) * (4 * groups), unroll=4)

    src_ref[...] = jnp.zeros_like(src_ref)
    for g in range(groups):
        for k in range(8):
            lanes = slice((8 * g + k) * LANES, (8 * g + k + 1) * LANES)
            for d in range(3):
                src_ref[RAW_S + d : RAW_S + d + 1, lanes] = found[4 * g + d][k : k + 1, :] - CENTRE
            src_ref[LOG_S : LOG_S + 1, lanes] = found[4 * g + 3][k : k + 1, :]
    square = jnp.zeros((1, n), jnp.float32)
    for d in range(3):
        raw = src_ref[RAW_S + d : RAW_S + d + 1, :]
        src_ref[d : d + 1, :] = ALPHA * raw
        square = square + raw * raw
    src_ref[BIAS_S : BIAS_S + 1, :] = -HALF * square
    src_ref[BIAS_T : BIAS_T + 1, :] = jnp.ones((1, n), jnp.float32)
    src_ref[LOG_S : LOG_S + 1, :] = jnp.log2(src_ref[LOG_S : LOG_S + 1, :])

    tiles = got_ref.shape[0]
    m = tgt_ref.shape[1]
    tgt_ref[...] = jnp.zeros_like(tgt_ref)
    flags = jnp.concatenate([got_ref[t][8:9, :] for t in range(tiles)] * 2, axis=0)
    src_tiles = n // TILE
    flags = pltpu.roll(flags, (LANES - quarter * src_tiles) % LANES, 1)
    bias = jnp.where(flags > 0.5, 0.0, LOWEST)
    for i in range(src_tiles):
        src_ref[MASK0 : MASK0 + tiles, i * TILE : (i + 1) * TILE] = jnp.broadcast_to(
            bias[:tiles, i : i + 1], (tiles, TILE)
        )
    mass = jnp.zeros((1, LANES), jnp.float32)
    for t in range(tiles):
        for k in range(2):
            lanes = slice(t * TILE + k * LANES, t * TILE + (k + 1) * LANES)
            square = jnp.zeros((1, LANES), jnp.float32)
            for d in range(3):
                raw = got_ref[t][2 * d + k : 2 * d + k + 1, :] - CENTRE
                tgt_ref[d : d + 1, lanes] = raw
                square = square + raw * raw
            tgt_ref[BIAS_T : BIAS_T + 1, lanes] = -HALF * square
            weight = got_ref[t][6 + k : 7 + k, :]
            tgt_ref[LOG_T : LOG_T + 1, lanes] = jnp.log2(weight)
            mass = mass + weight
        tgt_ref[MASK0 + t : MASK0 + t + 1, t * TILE : (t + 1) * TILE] = jnp.ones(
            (1, TILE), jnp.float32
        )
    tgt_ref[BIAS_S : BIAS_S + 1, :] = jnp.ones((1, m), jnp.float32)

    tgt = tgt_ref[...]
    bias_t = tgt_ref[BIAS_T : BIAS_T + 1, :] + tgt_ref[LOG_T : LOG_T + 1, :]
    left_side(with_row(tgt, BIAS_T, bias_t), left_ref)
    right_side(src_ref[...], right_ref)
    copies = out_ref.shape[0]

    def emit(at, value):
        out_ref[:, pl.ds(at, TILE)] = jnp.broadcast_to(value, (copies, TILE))

    row_pass(left_ref, right_ref, emit)
    whole = jnp.sum(mass, axis=1, keepdims=True)
    out_ref[:, n:] = jnp.broadcast_to(whole, (copies, LANES))


def first_cols(got_ref, src_ref, tgt_ref, field_ref, out_ref, left_ref, right_ref, top_ref, sum_ref):
    n = src_ref.shape[1]
    m = tgt_ref.shape[1]
    tgt_total = jnp.log2(jnp.sum(got_ref[:, n:], axis=0, keepdims=True))
    field = -(merged(got_ref[:, :n]) - tgt_total[:, :1])
    field_ref[0:1, :] = field
    field_ref[1:2, :] = jnp.broadcast_to(tgt_total[:, :1], (1, n))
    left_side(tgt_ref[...], left_ref)
    log_mass = src_ref[LOG_S : LOG_S + 1, :]
    bias = src_ref[BIAS_S : BIAS_S + 1, :] + log_mass
    copies = out_ref.shape[0]
    for k, term in enumerate((bias, bias + field)):
        right_side(with_row(src_ref[...], BIAS_S, term), right_ref)
        value = col_pass(left_ref, right_ref, top_ref, sum_ref)
        out_ref[:, k * m : (k + 1) * m] = jnp.broadcast_to(value, (copies, m))
    mass = jnp.sum(jnp.exp2(log_mass), axis=1, keepdims=True)
    out_ref[:, 2 * m :] = jnp.broadcast_to(mass, (copies, LANES))


def middle_rows(got_ref, src_ref, tgt_ref, field_ref, out_ref, left_ref, right_ref):
    n = src_ref.shape[1]
    m = tgt_ref.shape[1]
    src_total = jnp.log2(jnp.sum(got_ref[:, 2 * m :], axis=0, keepdims=True))[:, :1]
    start = -(merged(got_ref[:, :m]) - src_total)
    once = 0.5 * (start - (merged(got_ref[:, m : 2 * m]) - src_total))
    field_ref[0:1, :] = once
    field_ref[1:2, :] = jnp.broadcast_to(src_total, (1, m))
    right_side(src_ref[...], right_ref)
    base = tgt_ref[BIAS_T : BIAS_T + 1, :] + tgt_ref[LOG_T : LOG_T + 1, :]
    copies = out_ref.shape[0]
    for k, term in enumerate((start, once)):
        left_side(with_row(tgt_ref[...], BIAS_T, base + term), left_ref)

        def emit(at, value, k=k):
            out_ref[:, pl.ds(k * n + at, TILE)] = jnp.broadcast_to(value, (copies, TILE))

        row_pass(left_ref, right_ref, emit)


def middle_cols(got_ref, src_ref, tgt_ref, field_ref, out_ref, left_ref, right_ref, top_ref, sum_ref):
    n = src_ref.shape[1]
    m = tgt_ref.shape[1]
    tgt_total = field_ref[1:2, :]
    once = 0.5 * (field_ref[0:1, :] - (merged(got_ref[:, :n]) - tgt_total))
    twice = 0.5 * (once - (merged(got_ref[:, n:]) - tgt_total))
    left_side(tgt_ref[...], left_ref)
    bias = src_ref[BIAS_S : BIAS_S + 1, :] + src_ref[LOG_S : LOG_S + 1, :]
    copies = out_ref.shape[0]
    for k, term in enumerate((once, twice)):
        right_side(with_row(src_ref[...], BIAS_S, bias + term), right_ref)
        value = col_pass(left_ref, right_ref, top_ref, sum_ref)
        out_ref[:, k * m : (k + 1) * m] = jnp.broadcast_to(value, (copies, m))


def last_rows(
    quarter_ref, got_ref, src_ref, tgt_ref, field_ref, scale_ref, out_ref, own_ref,
    left_ref, right_ref, pull_ref, line_ref,
):
    n = src_ref.shape[1]
    m = tgt_ref.shape[1]
    src_total = field_ref[1:2, :]
    twice = 0.5 * (field_ref[0:1, :] - (merged(got_ref[:, :m]) - src_total))
    line_ref[...] = -UNIT * (merged(got_ref[:, m:]) - src_total)
    own_ref[...] = line_ref[:, pl.ds(pl.multiple_of(quarter_ref[0] * TILE, TILE), TILE)]
    right_side(src_ref[...], right_ref)
    base = tgt_ref[BIAS_T : BIAS_T + 1, :] + tgt_ref[LOG_T : LOG_T + 1, :]
    left_side(with_row(tgt_ref[...], BIAS_T, base + twice), left_ref)
    for d in range(3):
        for c in range(m // LANES):
            lanes = slice(c * LANES, (c + 1) * LANES)
            wide = jnp.broadcast_to(tgt_ref[d : d + 1, lanes], (LANES, LANES))
            pull_ref[d, lanes, :] = wide.T
    tgt_total = scale_ref[1:2, 0:1]
    share = n // out_ref.shape[0]
    pulls = [pull_ref[d] for d in range(3)]

    def emit(at, found):
        value, means = found
        piece = at // share
        lane = pl.multiple_of(at - piece * share, TILE)
        out_ref[pl.ds(piece, 1), 0:1, pl.ds(lane, TILE)] = (value - tgt_total)[None]
        for d in range(3):
            raw = src_ref[RAW_S + d : RAW_S + d + 1, pl.ds(at, TILE)]
            out_ref[pl.ds(piece, 1), d + 1 : d + 2, pl.ds(lane, TILE)] = (raw - means[d])[None]

    row_pass(left_ref, right_ref, emit, pull_refs=pulls)


def closing(got_ref, out_ref):
    values = got_ref[:, 0, :]
    peak = jnp.max(values, axis=0, keepdims=True)
    weight = jnp.exp2(values - peak)
    total = jnp.sum(weight, axis=0, keepdims=True)
    lines = [-UNIT * (peak + jnp.log2(total))]
    for d in range(3):
        lines.append(jnp.sum(weight * got_ref[:, d + 1, :], axis=0, keepdims=True) / total)
    both = jnp.concatenate(lines, axis=0)
    for k in range(out_ref.shape[0]):
        out_ref[k] = both


def spread(got_ref, value_ref, shift_ref):
    share = got_ref.shape[2]
    for k in range(got_ref.shape[0]):
        lanes = slice(k * share, (k + 1) * share)
        value_ref[:, lanes] = got_ref[k][0:1, :]
        shift_ref[:, lanes] = got_ref[k][1:4, :]


def exchange(array, axes):
    return lax.all_to_all(array, axes, 0, 0, tiled=True)


def local(src_pos, tgt_pos, src_weight, tgt_weight, src_order, tgt_order, tile_mask):
    rows_here = src_pos.shape[1]
    splits = lax.axis_size(SPLIT)
    merges = lax.axis_size(MERGE)
    heights = lax.axis_size((ROW,) + SPLIT)
    n = rows_here // splits
    m = tgt_pos.shape[1] * splits
    quarter = lax.axis_index(SPLIT).astype(jnp.int32).reshape(1)
    left = pltpu.VMEM((m, LANES), jnp.bfloat16)
    right = pltpu.VMEM((LANES, n), jnp.bfloat16)
    wide = pltpu.VMEM((m, LANES), jnp.float32)

    packed = call(pack_targets, f32((splits, 16, LANES)))(
        tgt_pos,
        tgt_weight.reshape(-1, LANES),
        tgt_order.reshape(-1, LANES),
        tile_mask,
    )
    packed = exchange(packed, SPLIT)
    src, tgt, row0 = call(
        first_rows, (f32((16, n)), f32((16, m)), f32((merges, n + LANES))), (left, right), (0,)
    )(quarter, packed, src_pos, src_weight.reshape(-1, LANES), src_order.reshape(-1, LANES))
    row0 = exchange(row0, MERGE)
    src_field, col01 = call(
        first_cols, (f32((2, n)), f32((heights, 2 * m + LANES))), (left, right, wide, wide)
    )(row0, src, tgt)
    col01 = exchange(col01, (ROW,) + SPLIT)
    tgt_field, row12 = call(middle_rows, (f32((2, m)), f32((merges, 2 * n))), (left, right))(
        col01, src, tgt
    )
    row12 = exchange(row12, MERGE)
    col23 = call(middle_cols, f32((heights, 2 * m)), (left, right, wide, wide))(
        row12, src, tgt, src_field
    )
    col23 = exchange(col23, (ROW,) + SPLIT)
    row3, own = call(
        last_rows,
        (f32((merges, 4, n // merges)), f32((1, TILE))),
        (left, right, pltpu.VMEM((3, m, LANES), jnp.float32), pltpu.VMEM((1, m), jnp.float32)),
        (0,),
    )(quarter, col23, src, tgt, tgt_field, src_field)
    row3 = exchange(row3, MERGE)
    everyone = SPLIT + MERGE
    done = call(closing, f32((lax.axis_size(everyone), 4, n // merges)))(row3)
    done = exchange(done, everyone)
    value, shift = call(spread, (f32((1, rows_here)), f32((3, rows_here))))(done)
    return value.reshape(-1), own.reshape(-1), shift


def solution(mesh):
    split = Mesh(mesh.devices.reshape(mesh.shape["row"], 4, 4, 2), ("row", "y", "x", "core"))
    in_specs = (P(None, ROW), P(None, COLS), P(ROW), P(COLS), P(ROW), P(COLS), P(ROW, COLS))
    out_specs = (P(ROW), P(COLS), P(None, ROW))
    return jax.shard_map(local, mesh=split, in_specs=in_specs, out_specs=out_specs, check_vma=False)
```

```python
import jax
import jax.numpy as jnp
from jax import lax
from jax.experimental import pallas as pl
from jax.experimental.pallas import tpu as pltpu
from jax.sharding import Mesh
from jax.sharding import PartitionSpec as P

epsilon = 0.4
LOG2E = 1.4426950408889634
LN2 = 0.6931471805599453
ALPHA = LOG2E / epsilon
HALF = 0.5 * ALPHA
UNIT = epsilon * LN2
CENTRE = 7.5
LOWEST = -(2.0**100)
TILE = 256
LANES = 128

ROW = "row"
SPLIT = ("x",)
MERGE = ("y", "core")
COLS = ("y", "x", "core")

BIAS_S, BIAS_T, MASK0, LOG_S, RAW_S, LOG_T = 3, 4, 5, 9, 10, 13


def f32(shape):
    return jax.ShapeDtypeStruct(shape, jnp.float32)


def call(body, outs, scratch=(), smem=()):
    def run(*args):
        specs = [
            pl.BlockSpec(memory_space=pltpu.SMEM if k in smem else pltpu.VMEM)
            for k in range(len(args))
        ]
        return pl.pallas_call(
            body,
            out_shape=outs,
            in_specs=specs,
            out_specs=jax.tree.map(lambda _: pl.BlockSpec(memory_space=pltpu.VMEM), outs),
            scratch_shapes=list(scratch),
            compiler_params=pltpu.CompilerParams(vmem_limit_bytes=48 << 20),
        )(*args)

    return run


def parts(u):
    hi = u.astype(jnp.bfloat16)
    rest = u - hi.astype(jnp.float32)
    mid = rest.astype(jnp.bfloat16)
    low = (rest - mid.astype(jnp.float32)).astype(jnp.bfloat16)
    return hi, mid, low


def right_side(u, out_ref):
    hi, mid, low = parts(u)
    zero = jnp.zeros_like(hi)
    out_ref[...] = jnp.concatenate([hi, mid, hi, mid, low, hi, zero, zero], axis=0)


def left_side(u, out_ref):
    hi, mid, low = (p.astype(jnp.float32) for p in parts(u))
    zero = jnp.zeros_like(hi)
    stacked = jnp.concatenate([hi, hi, mid, mid, hi, low, zero, zero], axis=0)
    for c in range(u.shape[1] // LANES):
        block = stacked[:, c * LANES : (c + 1) * LANES]
        out_ref[c * LANES : (c + 1) * LANES, :] = block.T.astype(jnp.bfloat16)


def with_row(u, at, row):
    rows = lax.broadcasted_iota(jnp.int32, u.shape, 0)
    return jnp.where(rows == at, row, u)


def pipelined(steps, fill, drain, buffers):
    one, two = buffers
    fill(0, *one)

    def pair(i, carry):
        fill(2 * i + 1, *two)
        drain(2 * i, *one)
        fill(jnp.minimum(2 * i + 2, steps - 1), *one)
        drain(2 * i + 1, *two)
        return carry

    lax.fori_loop(0, steps // 2, pair, 0)


def row_pass(left_ref, right_ref, buffers, emit, pull_ref=None):
    def fill(b, x_ref, top_ref):
        at = pl.multiple_of(b * TILE, TILE)
        x = jnp.dot(
            left_ref[...], right_ref[:, pl.ds(at, TILE)], preferred_element_type=jnp.float32
        )
        x_ref[...] = x
        top_ref[...] = jnp.max(x.reshape(-1, 8, TILE), axis=0)

    def drain(b, x_ref, top_ref):
        top = top_ref[...]
        p = jnp.exp2(x_ref[...].reshape(-1, 8, TILE) - top[None])
        total = jnp.sum(p, axis=0)
        peak = jnp.max(top, axis=0, keepdims=True)
        weight = jnp.exp2(top - peak)
        sums = jnp.sum(total * weight, axis=0, keepdims=True)
        lines = [peak + jnp.log2(sums)]
        if pull_ref is not None:
            for d in range(3):
                wide = pull_ref[d]
                wide = jnp.concatenate([wide] * (TILE // LANES), axis=1)
                moved = jnp.sum(p * wide.reshape(-1, 8, TILE), axis=0)
                lines.append(jnp.sum(moved * weight, axis=0, keepdims=True) / sums)
        for k in range(TILE // LANES):
            emit(
                b * (TILE // LANES) + k,
                [line[:, k * LANES : (k + 1) * LANES] for line in lines],
            )

    pipelined(right_ref.shape[1] // TILE, fill, drain, buffers)


def col_pass(left_ref, right_ref, buffers, top_ref, sum_ref):
    m = left_ref.shape[0]
    width = buffers[0][0].shape[1]
    cuts = [slice(k * LANES, (k + 1) * LANES) for k in range(width // LANES)]
    blocks = right_ref.shape[1] // width
    top_ref[...] = jnp.full(top_ref.shape, 2.0 * LOWEST, jnp.float32)
    sum_ref[...] = jnp.zeros(sum_ref.shape, jnp.float32)

    def place(s):
        t = s // blocks
        return pl.multiple_of(t * TILE, TILE), pl.multiple_of((s - t * blocks) * width, width)

    def fill(s, x_ref, peak_ref):
        row, at = place(s)
        x = jnp.dot(
            left_ref[pl.ds(row, TILE), :],
            right_ref[:, pl.ds(at, width)],
            preferred_element_type=jnp.float32,
        )
        x_ref[...] = x
        peak = x[:, cuts[0]]
        for cut in cuts[1:]:
            peak = jnp.maximum(peak, x[:, cut])
        peak_ref[...] = peak

    def drain(s, x_ref, peak_ref):
        row, _ = place(s)
        old = top_ref[pl.ds(row, TILE), :]
        top = jnp.maximum(old, peak_ref[...])
        total = sum_ref[pl.ds(row, TILE), :] * jnp.exp2(old - top)
        for cut in cuts:
            total = total + jnp.exp2(x_ref[:, cut] - top)
        top_ref[pl.ds(row, TILE), :] = top
        sum_ref[pl.ds(row, TILE), :] = total

    pipelined((m // TILE) * blocks, fill, drain, buffers)
    found = []
    for c in range(m // LANES):
        top = top_ref[c * LANES : (c + 1) * LANES, :].T
        total = sum_ref[c * LANES : (c + 1) * LANES, :].T
        peak = jnp.max(top, axis=0, keepdims=True)
        sums = jnp.sum(total * jnp.exp2(top - peak), axis=0, keepdims=True)
        found.append(peak + jnp.log2(sums))
    return jnp.concatenate(found, axis=0)


def merged(values):
    peak = jnp.max(values, axis=0)
    return peak + jnp.log2(jnp.sum(jnp.exp2(values - peak[None]), axis=0))


def total_of(pieces):
    return jnp.log2(jnp.sum(pieces, axis=0))


def flat_add(u_ref, row, lines, base=None):
    for c in range(lines.shape[0]):
        lanes = slice(c * LANES, (c + 1) * LANES)
        line = lines[c : c + 1, :]
        if base is not None:
            line = line + base[:, lanes]
        u_ref[row : row + 1, lanes] = line


def mirrored(out_ref, lines):
    for k in range(out_ref.shape[0]):
        out_ref[k] = lines


def run_cols(src_ref, tgt_ref, out_ref, field, work):
    u_ref, left_ref, right_ref, one, two, peak_one, peak_two, top_ref, sum_ref = work
    left_side(tgt_ref[...], left_ref)
    log_mass = src_ref[LOG_S : LOG_S + 1, :]
    bias = src_ref[BIAS_S : BIAS_S + 1, :] + log_mass
    u_ref[...] = src_ref[...]
    if field is None:
        u_ref[BIAS_S : BIAS_S + 1, :] = bias
    else:
        flat_add(u_ref, BIAS_S, field, bias)
    right_side(u_ref[...], right_ref)
    buffers = ((one, peak_one), (two, peak_two))
    return col_pass(left_ref, right_ref, buffers, top_ref, sum_ref)


def run_rows(src_ref, tgt_ref, emit, field, work, pull_ref=None):
    u_ref, left_ref, right_ref, one, two, peak_one, peak_two = work
    base = tgt_ref[BIAS_T : BIAS_T + 1, :] + tgt_ref[LOG_T : LOG_T + 1, :]
    u_ref[...] = tgt_ref[...]
    if field is None:
        u_ref[BIAS_T : BIAS_T + 1, :] = base
    else:
        flat_add(u_ref, BIAS_T, field, base)
    left_side(u_ref[...], left_ref)
    right_side(src_ref[...], right_ref)
    buffers = ((one, peak_one), (two, peak_two))
    row_pass(left_ref, right_ref, buffers, emit, pull_ref)


def to_lines(line_ref):
    def emit(at, found):
        line_ref[pl.ds(at, 1), :] = found[0]

    return emit


def lane_gather(table, lanes):
    return jnp.take_along_axis(table, lanes, axis=1, mode="promise_in_bounds")


def pack_targets(pos_ref, weight_ref, order_ref, mask_ref, out_ref):
    order = jnp.bitwise_and(order_ref[...], TILE - 1)
    high = jnp.right_shift(order, 7)
    low = jnp.bitwise_and(order, LANES - 1)
    high8 = jnp.concatenate([high] * 4, axis=0)
    low8 = jnp.concatenate([low] * 4, axis=0)
    found = jnp.zeros((8, LANES), jnp.float32)
    for r in range(2):
        lanes = slice(r * LANES, (r + 1) * LANES)
        lines = [jnp.broadcast_to(pos_ref[d : d + 1, lanes], (2, LANES)) for d in range(3)]
        lines.append(jnp.broadcast_to(weight_ref[r : r + 1, :], (2, LANES)))
        table = jnp.concatenate(lines, axis=0)
        found = jnp.where(high8 == r, lane_gather(table, low8), found)
    tiles = mask_ref.shape[0]
    at = lax.broadcasted_iota(jnp.int32, (tiles, LANES), 0)
    lane = lax.broadcasted_iota(jnp.int32, (tiles, LANES), 1)
    kept = jnp.broadcast_to(mask_ref[...].astype(jnp.float32), (tiles, LANES))
    line = jnp.sum(jnp.where(at == lane, kept, 0.0), axis=0, keepdims=True)
    both = jnp.concatenate([found, jnp.broadcast_to(line, (8, LANES))], axis=0)
    for k in range(out_ref.shape[0]):
        out_ref[k] = both


def source_features(quarter_ref, pos_ref, weight_ref, order_ref, src_ref):
    quarter = quarter_ref[0]
    n = src_ref.shape[1]
    lines = n // LANES
    groups = lines // 8
    order = order_ref[pl.ds(pl.multiple_of(quarter * lines, 8), lines), :]
    order = jnp.bitwise_and(order, LANES * LANES - 1)
    high = jnp.right_shift(order, 7)
    low = jnp.bitwise_and(order, LANES - 1)
    highs = [high[8 * g : 8 * g + 8] for g in range(groups)]
    lows = [low[8 * g : 8 * g + 8] for g in range(groups)]

    def look(r, found):
        at = pl.multiple_of(r * LANES, LANES)
        tables = [
            jnp.broadcast_to(pos_ref[d : d + 1, pl.ds(at, LANES)], (8, LANES)) for d in range(3)
        ]
        tables.append(jnp.broadcast_to(weight_ref[pl.ds(r, 1), :], (8, LANES)))
        out = []
        for g in range(groups):
            here = highs[g] == r
            for a in range(4):
                old = found[4 * g + a]
                out.append(jnp.where(here, lane_gather(tables[a], lows[g]), old))
        return tuple(out)

    zero = jnp.zeros((8, LANES), jnp.float32)
    found = lax.fori_loop(0, LANES, look, (zero,) * (4 * groups), unroll=4)

    src_ref[...] = jnp.zeros_like(src_ref)
    for g in range(groups):
        square = jnp.zeros((8, LANES), jnp.float32)
        raw = []
        for d in range(3):
            raw.append(found[4 * g + d] - CENTRE)
            square = square + raw[d] * raw[d]
        rows = {LOG_S: jnp.log2(found[4 * g + 3]), BIAS_S: -HALF * square}
        for d in range(3):
            rows[RAW_S + d] = raw[d]
            rows[d] = ALPHA * raw[d]
        for row, values in rows.items():
            for k in range(8):
                lanes = slice((8 * g + k) * LANES, (8 * g + k + 1) * LANES)
                src_ref[row : row + 1, lanes] = values[k : k + 1, :]
    src_ref[BIAS_T : BIAS_T + 1, :] = jnp.ones((1, n), jnp.float32)


def opening_cols(quarter_ref, got_ref, part_ref, src_ref, tgt_ref, out_ref, *work):
    n = src_ref.shape[1]
    m = tgt_ref.shape[1]
    tiles = got_ref.shape[0]
    flags = jnp.concatenate([got_ref[t][8:9, :] for t in range(tiles)] * 2, axis=0)
    src_tiles = n // TILE
    flags = pltpu.roll(flags, (LANES - quarter_ref[0] * src_tiles) % LANES, 1)
    bias = jnp.where(flags > 0.5, 0.0, LOWEST)
    src_ref[...] = part_ref[...]
    for i in range(src_tiles):
        src_ref[MASK0 : MASK0 + tiles, i * TILE : (i + 1) * TILE] = jnp.broadcast_to(
            bias[:tiles, i : i + 1], (tiles, TILE)
        )
    tgt_ref[...] = jnp.zeros_like(tgt_ref)
    for t in range(tiles):
        for k in range(2):
            lanes = slice(t * TILE + k * LANES, t * TILE + (k + 1) * LANES)
            square = jnp.zeros((1, LANES), jnp.float32)
            for d in range(3):
                raw = got_ref[t][2 * d + k : 2 * d + k + 1, :] - CENTRE
                tgt_ref[d : d + 1, lanes] = raw
                square = square + raw * raw
            tgt_ref[BIAS_T : BIAS_T + 1, lanes] = -HALF * square
            tgt_ref[LOG_T : LOG_T + 1, lanes] = jnp.log2(got_ref[t][6 + k : 7 + k, :])
        tgt_ref[MASK0 + t : MASK0 + t + 1, t * TILE : (t + 1) * TILE] = jnp.ones(
            (1, TILE), jnp.float32
        )
    tgt_ref[BIAS_S : BIAS_S + 1, :] = jnp.ones((1, m), jnp.float32)
    value = run_cols(src_ref, tgt_ref, out_ref, None, work)
    mass = jnp.sum(jnp.exp2(src_ref[LOG_S : LOG_S + 1, :]), axis=1, keepdims=True)
    mirrored(out_ref, jnp.concatenate([value, jnp.broadcast_to(mass, (8, LANES))], axis=0))


def opening_rows(src_ref, tgt_ref, out_ref, line_ref, *work):
    n = src_ref.shape[1]
    run_rows(src_ref, tgt_ref, to_lines(line_ref), None, work)
    mass = jnp.sum(jnp.exp2(tgt_ref[LOG_T : LOG_T + 1, :]), axis=1, keepdims=True)
    line_ref[n // LANES :, :] = jnp.broadcast_to(mass, (8, LANES))
    mirrored(out_ref, line_ref[...])


def second_cols(got_ref, src_ref, tgt_ref, field_ref, out_ref, *work):
    lines = src_ref.shape[1] // LANES
    total = total_of(got_ref[:, lines:, :])
    field = -(merged(got_ref[:, :lines, :]) - total[:1, :1])
    field_ref[:lines, :] = field
    field_ref[lines:, :] = total
    mirrored(out_ref, run_cols(src_ref, tgt_ref, out_ref, field, work))


def second_rows(got_ref, src_ref, tgt_ref, field_ref, out_ref, line_ref, *work):
    lines = tgt_ref.shape[1] // LANES
    total = total_of(got_ref[:, lines:, :])
    field = -(merged(got_ref[:, :lines, :]) - total[:1, :1])
    field_ref[:lines, :] = field
    field_ref[lines:, :] = total
    run_rows(src_ref, tgt_ref, to_lines(line_ref), field, work)
    mirrored(out_ref, line_ref[...])


def updated(got_ref, field_ref):
    lines = field_ref.shape[0] - 8
    total = field_ref[lines:, :]
    return 0.5 * (field_ref[:lines, :] - (merged(got_ref[...]) - total[:1, :1])), total


def sweep_cols(got_ref, old_ref, src_ref, tgt_ref, field_ref, out_ref, *work):
    field, total = updated(got_ref, old_ref)
    field_ref[: field.shape[0], :] = field
    field_ref[field.shape[0] :, :] = total
    mirrored(out_ref, run_cols(src_ref, tgt_ref, out_ref, field, work))


def sweep_rows(got_ref, old_ref, src_ref, tgt_ref, field_ref, out_ref, line_ref, *work):
    field, total = updated(got_ref, old_ref)
    field_ref[: field.shape[0], :] = field
    field_ref[field.shape[0] :, :] = total
    run_rows(src_ref, tgt_ref, to_lines(line_ref), field, work)
    mirrored(out_ref, line_ref[...])


def last_rows(got_ref, old_ref, scale_ref, src_ref, tgt_ref, out_ref, pull_ref, *work):
    field, _ = updated(got_ref, old_ref)
    for d in range(3):
        for c in range(tgt_ref.shape[1] // LANES):
            lanes = slice(c * LANES, (c + 1) * LANES)
            wide = jnp.broadcast_to(tgt_ref[d : d + 1, lanes], (LANES, LANES))
            pull_ref[d, lanes, :] = wide.T
    lines = src_ref.shape[1] // LANES
    total = scale_ref[lines : lines + 1, 0:1]
    share = lines // out_ref.shape[0]

    def emit(at, found):
        piece = at // share
        row = at - piece * share
        out_ref[piece, pl.ds(row, 1), :] = found[0] - total
        lanes = pl.ds(pl.multiple_of(at * LANES, LANES), LANES)
        for d in range(3):
            raw = src_ref[RAW_S + d : RAW_S + d + 1, lanes]
            out_ref[piece, pl.ds(row + (d + 1) * share, 1), :] = raw - found[d + 1]

    run_rows(src_ref, tgt_ref, emit, field, work, pull_ref)


def closing(got_ref, out_ref):
    share = got_ref.shape[1] // 4
    values = got_ref[:, :share, :]
    peak = jnp.max(values, axis=0)
    weight = jnp.exp2(values - peak[None])
    total = jnp.sum(weight, axis=0)
    lines = [-UNIT * (peak + jnp.log2(total))]
    for d in range(3):
        piece = got_ref[:, (d + 1) * share : (d + 2) * share, :]
        lines.append(jnp.sum(weight * piece, axis=0) / total)
    mirrored(out_ref, jnp.concatenate(lines, axis=0))


def spread(quarter_ref, got_ref, col_ref, scale_ref, value_ref, shift_ref, own_ref, line_ref):
    share = got_ref.shape[1] // 4
    for k in range(got_ref.shape[0]):
        for r in range(share):
            lanes = slice((k * share + r) * LANES, (k * share + r + 1) * LANES)
            value_ref[:, lanes] = got_ref[k][r : r + 1, :]
            for d in range(3):
                row = (d + 1) * share + r
                shift_ref[d : d + 1, lanes] = got_ref[k][row : row + 1, :]
    lines = col_ref.shape[1]
    total = scale_ref[lines : lines + 1, 0:1]
    line_ref[...] = -UNIT * (merged(col_ref[...]) - total)
    for k in range(2):
        row = 2 * quarter_ref[0] + k
        own_ref[:, k * LANES : (k + 1) * LANES] = line_ref[pl.ds(row, 1), :]


def exchange(array, axes):
    return lax.all_to_all(array, axes, 0, 0, tiled=True)


def local(src_pos, tgt_pos, src_weight, tgt_weight, src_order, tgt_order, tile_mask):
    rows_here = src_pos.shape[1]
    splits = lax.axis_size(SPLIT)
    merges = lax.axis_size(MERGE)
    heights = lax.axis_size((ROW,) + SPLIT)
    everyone = SPLIT + MERGE
    n = rows_here // splits
    m = tgt_pos.shape[1] * splits
    nl, ml = n // LANES, m // LANES
    quarter = lax.axis_index(SPLIT).astype(jnp.int32).reshape(1)
    left = pltpu.VMEM((m, LANES), jnp.bfloat16)
    right = pltpu.VMEM((LANES, n), jnp.bfloat16)

    def vm(*shape):
        return pltpu.VMEM(shape, jnp.float32)

    wide = 1024
    col_work = (vm(16, n), left, right, vm(TILE, wide), vm(TILE, wide))
    col_work += (vm(TILE, LANES), vm(TILE, LANES), vm(m, LANES), vm(m, LANES))
    row_work = (vm(16, m), left, right, vm(m, TILE), vm(m, TILE), vm(8, TILE), vm(8, TILE))
    src_shape, tgt_shape = f32((16, n)), f32((16, m))
    field_s, field_t = f32((nl + 8, LANES)), f32((ml + 8, LANES))
    to_cols, to_rows = f32((heights, ml, LANES)), f32((merges, nl, LANES))
    heads = (ROW,) + SPLIT

    packed = call(pack_targets, f32((splits, 16, LANES)))(
        tgt_pos, tgt_weight.reshape(-1, LANES), tgt_order.reshape(-1, LANES), tile_mask
    )
    packed = exchange(packed, SPLIT)
    part = call(source_features, src_shape, (), (0,))(
        quarter, src_pos, src_weight.reshape(-1, LANES), src_order.reshape(-1, LANES)
    )
    src, tgt, col0 = call(
        opening_cols, (src_shape, tgt_shape, f32((heights, ml + 8, LANES))), col_work, (0,)
    )(quarter, packed, part)
    col0 = exchange(col0, heads)
    row0 = call(opening_rows, f32((merges, nl + 8, LANES)), (vm(nl + 8, LANES),) + row_work)(
        src, tgt
    )
    row0 = exchange(row0, MERGE)
    f0, col1 = call(second_cols, (field_s, to_cols), col_work)(row0, src, tgt)
    col1 = exchange(col1, heads)
    line = (vm(nl, LANES),)
    g0, row1 = call(second_rows, (field_t, to_rows), line + row_work)(col0, src, tgt)
    row1 = exchange(row1, MERGE)
    g1, row2 = call(sweep_rows, (field_t, to_rows), line + row_work)(col1, g0, src, tgt)
    row2 = exchange(row2, MERGE)
    f1, col2 = call(sweep_cols, (field_s, to_cols), col_work)(row1, f0, src, tgt)
    col2 = exchange(col2, heads)
    _, col3 = call(sweep_cols, (field_s, to_cols), col_work)(row2, f1, src, tgt)
    col3 = exchange(col3, heads)
    row3 = call(last_rows, f32((merges, 4 * (nl // merges), LANES)), (vm(3, m, LANES),) + row_work)(
        col2, g1, f1, src, tgt
    )
    row3 = exchange(row3, MERGE)
    done = call(closing, f32((lax.axis_size(everyone), 4 * (nl // merges), LANES)))(row3)
    done = exchange(done, everyone)
    value, shift, own = call(
        spread, (f32((1, rows_here)), f32((3, rows_here)), f32((1, TILE))), (vm(ml, LANES),), (0,)
    )(quarter, done, col3, g1)
    return value.reshape(-1), own.reshape(-1), shift


def solution(mesh):
    split = Mesh(mesh.devices.reshape(mesh.shape["row"], 4, 4, 2), ("row", "y", "x", "core"))
    in_specs = (P(None, ROW), P(None, COLS), P(ROW), P(COLS), P(ROW), P(COLS), P(ROW, COLS))
    out_specs = (P(ROW), P(COLS), P(None, ROW))
    return jax.shard_map(local, mesh=split, in_specs=in_specs, out_specs=out_specs, check_vma=False)
```
